256 devices in a mesh: tm: 16 (over x, z_hi, core), input: 16 (over z_lo, y).
Axes of the slice: x: 4, y: 4, z: 8 (z_hi: 2, z_lo: 4; z = z_hi * 4 + z_lo), core: 2. Of those that a mesh axis runs over, the one named last changes fastest.
Arguments:
- samples: bfloat16 [2, 262144, 2048], P(None, 'tm', 'input'), may hold values from -6 to 6
- filter_taps: float32 [16, 1024], replicated, may hold values from -1.5 to 1.5
Outputs:
- visibilities: bfloat16 [2, 64, 2048, 2048], P(None, 'tm', 'input')
The draws below stay inside these ranges and needn't reach their ends.
All inputs are finite; a program needn't handle non-finite values.
Results may differ from the reference program's by a relative error of at most 0.0056.
Values may be sent and summed in bfloat16 or wider, within the bound.
A program may use at most 192 MiB of HBM per device.

```python
import jax
import jax.numpy as jnp
from jax import lax

NCH = 1024
TAPS = 16
INP_DEV = 128
SUB = 64
FRAMES = 256
SAMPLES = 262144
INPUTS = 2048


def level_of(key, extent, cuts, low, high):
    gain = 1.0
    for dim, blocks in cuts:
        heights = jax.random.uniform(jax.random.fold_in(jax.random.fold_in(key, 6), dim), (blocks,), jnp.float32, low / len(cuts), high / len(cuts))
        gain = gain * jnp.repeat(jnp.exp(heights), extent[dim] // blocks).reshape((-1,) + (1,) * (len(extent) - 1 - dim))
    return gain


def normal_values(own_key, dims, width, limit, shards=(), kind=jnp.bfloat16):
    drawn = width * jax.random.normal(own_key, dims, jnp.float32)
    if shards:
        drawn = drawn * level_of(own_key, dims, shards, -0.22, 0.18)
    return jnp.clip(drawn, -limit, limit).astype(kind)


def setup_inputs(seed: int = 0) -> dict:
    key_list = jax.random.split(jax.random.key(seed), 3)
    samples = normal_values(key_list[0], (2, SAMPLES, INPUTS), 1.0, 6.0, ((1, 16), (2, 16)))
    filter_taps = normal_values(key_list[1], (TAPS, NCH), TAPS ** -0.5, 1.5, (), jnp.float32)
    return {"samples": samples, "filter_taps": filter_taps}


def dft_table(count, length):
    chan = jnp.arange(count, dtype=jnp.int32)
    point = jnp.arange(length, dtype=jnp.int32)
    phase = chan[:, None] * point[None, :] % length
    theta = 2.0 * jnp.pi / length * phase.astype(jnp.float32)
    scale = 1.0 / jnp.sqrt(jnp.float32(length))
    cosine = jnp.cos(theta) * scale
    sine = jnp.sin(theta) * scale
    real_rows = jnp.stack([cosine, sine], axis=1)
    imag_rows = jnp.stack([-sine, cosine], axis=1)
    return jnp.concatenate([real_rows, imag_rows], axis=0)

def reference(samples, filter_taps):
    framed = samples.reshape(2, FRAMES, NCH, INPUTS)
    table = dft_table(SUB, NCH)
    blocks = INPUTS // INP_DEV

    def one_block(index):
        start = (index * INP_DEV).astype(jnp.int32)
        block = lax.dynamic_slice_in_dim(framed, start, INP_DEV, 3)
        padded = jnp.concatenate([block, jnp.zeros((2, TAPS - 1, NCH, INP_DEV), jnp.bfloat16)], axis=1)
        filtered = jnp.zeros((2, FRAMES, NCH, INP_DEV), jnp.float32)
        for tap in range(TAPS):
            filtered = filtered + filter_taps[tap][None, None, :, None] * padded[:, tap:tap + FRAMES].astype(jnp.float32)
        spectra = jnp.einsum('kcn,cfna->kfa', table, filtered, precision=lax.Precision.HIGHEST)
        return spectra.reshape(2, SUB, FRAMES, INP_DEV).astype(jnp.bfloat16)
    parts = lax.map(one_block, jnp.arange(blocks, dtype=jnp.int32))
    spectra = jnp.moveaxis(parts, 0, 3).reshape(2, SUB, FRAMES, INPUTS)

    def one_channel(chan):
        real_part = spectra[0, chan]
        imag_part = spectra[1, chan]
        real_out = jnp.dot(real_part.T, real_part, preferred_element_type=jnp.float32) + jnp.dot(imag_part.T, imag_part, preferred_element_type=jnp.float32)
        imag_out = jnp.dot(imag_part.T, real_part, preferred_element_type=jnp.float32) - jnp.dot(real_part.T, imag_part, preferred_element_type=jnp.float32)
        return (jnp.stack([real_out, imag_out]) * (1.0 / FRAMES)).astype(jnp.bfloat16)
    result = lax.map(one_channel, jnp.arange(SUB, dtype=jnp.int32))
    return jnp.moveaxis(result, 0, 1)
```

```python
import functools

import jax
import jax.numpy as jnp
import numpy as np
from jax import lax
from jax.experimental import pallas as pl
from jax.experimental.pallas import tpu as pltpu
from jax.sharding import PartitionSpec as P

MESH = pl.DeviceIdType.MESH
CH_DEV = 4
TM = 16
NY = 4
NZ = 4
INP = NY * NZ


def trig_table(nch):
    chan = CH_DEV * np.arange(TM)[None, :] + np.arange(CH_DEV)[:, None]
    phase = chan[:, :, None] * np.arange(nch)[None, None, :] % nch
    theta = 2.0 * np.pi / nch * phase
    scale = 1.0 / np.sqrt(nch)
    return np.stack([np.cos(theta) * scale, np.sin(theta) * scale]).astype(np.float32)


def kernel(x_hbm, taps_ref, trig_ref, out_hbm, xv, ghi, glo, acc, part, recv, blocks, lt, vout,
           x_sem, turn_send, turn_recv, z_send, z_recv, y_send, y_recv, f_send, f_recv, out_sem):
    t = lax.axis_index("tm")
    i = lax.axis_index("input")
    z = i // NY
    y = lax.rem(i, NY)
    up = lax.rem(y + 1, NY)
    down = lax.rem(y + NY - 1, NY)
    ntaps, nch = taps_ref.shape
    frames = xv.shape[1]
    width = xv.shape[3]
    rows = 2 * TM
    pairs = frames // 2

    def x_copy(p):
        sl = pl.ds(2 * p, 2)
        return pltpu.make_async_copy(x_hbm.at[:, sl], xv.at[:, sl], x_sem.at[p])

    for p in range(pairs):
        x_copy(p).start()

    barrier = pltpu.get_barrier_semaphore()

    @pl.loop(1, TM)
    def _(d):
        pl.semaphore_signal(barrier, inc=1, device_id={"tm": lax.rem(t + d, TM), "input": i}, device_id_type=MESH)

    for d in range(1, NZ):
        pl.semaphore_signal(
            barrier, inc=1, device_id={"tm": t, "input": lax.rem(z + d, NZ) * NY + y}, device_id_type=MESH)
    for side in (up, down):
        pl.semaphore_signal(barrier, inc=1, device_id={"tm": t, "input": z * NY + side}, device_id_type=MESH)

    def weights(c):
        cosine = trig_ref[0, c]
        sine = trig_ref[1, c]

        @pl.loop(0, ntaps)
        def _(tap):
            h = taps_ref[pl.ds(tap, 1), :]
            co = cosine * h
            si = sine * h
            for r0, c0, val in ((0, 0, co), (0, nch, si), (TM, 0, -si), (TM, nch, co)):
                at = pl.multiple_of(tap * rows + r0, TM)
                hi = val.astype(jnp.bfloat16)
                ghi[pl.ds(at, TM), c0:c0 + nch] = hi
                glo[pl.ds(at, TM), c0:c0 + nch] = (val - hi.astype(jnp.float32)).astype(jnp.bfloat16)

        acc[...] = jnp.zeros_like(acc)

    def filtered(c, lo, hi):
        @pl.loop(lo, hi)
        def _(p):
            if c == 0:
                x_copy(p).wait()
            b0 = jnp.concatenate([xv[0, 2 * p], xv[0, 2 * p + 1]], axis=1)
            b1 = jnp.concatenate([xv[1, 2 * p], xv[1, 2 * p + 1]], axis=1)
            both = jnp.concatenate([b0, b1], axis=0)
            prod = jnp.dot(ghi[...], both, preferred_element_type=jnp.float32)
            prod = prod + jnp.dot(glo[...], both, preferred_element_type=jnp.float32)
            for tap in range(ntaps):
                for j in range(2):
                    at = pl.ds(pl.multiple_of((2 * p + j - tap + frames) * rows, rows), rows)
                    acc[at, :] += prod[tap * rows:(tap + 1) * rows, j * width:(j + 1) * width]

    def finish(c):
        for part_index in range(2):
            for owner in range(TM):
                r = part_index * TM + owner
                part[c, owner, part_index] = acc[pl.ds(r, rows, stride=rows), :].astype(jnp.bfloat16)
        recv[c, t] = part[c, t]

    def turn_copy(c, d):
        owner = lax.rem(t + d, TM)
        return pltpu.make_async_remote_copy(
            src_ref=part.at[c, owner], dst_ref=recv.at[c, t],
            send_sem=turn_send.at[c, d], recv_sem=turn_recv.at[c, d],
            device_id={"tm": owner, "input": i}, device_id_type=MESH)

    def turn_start(c):
        @pl.loop(1, TM)
        def _(d):
            turn_copy(c, d).start()

    def z_copy(c, d):
        return pltpu.make_async_remote_copy(
            src_ref=blocks.at[c, i], dst_ref=blocks.at[c, i],
            send_sem=z_send.at[c, d], recv_sem=z_recv.at[c, d],
            device_id={"tm": t, "input": lax.rem(z + d, NZ) * NY + y}, device_id_type=MESH)

    def y_copy(c, d, side):
        slot = lax.rem(z + NZ - d, NZ) * NY + y
        return pltpu.make_async_remote_copy(
            src_ref=blocks.at[c, slot], dst_ref=blocks.at[c, slot],
            send_sem=y_send.at[c, side, d], recv_sem=y_recv.at[c, side, d],
            device_id={"tm": t, "input": z * NY + (up, down)[side]}, device_id_type=MESH)

    def f_copy(c, d, side):
        slot = lax.rem(z + NZ - d, NZ) * NY + (down, up)[side]
        return pltpu.make_async_remote_copy(
            src_ref=blocks.at[c, slot, side], dst_ref=blocks.at[c, slot, side],
            send_sem=f_send.at[c, side, d], recv_sem=f_recv.at[c, side, d],
            device_id={"tm": t, "input": z * NY + (up, down)[side]}, device_id_type=MESH)

    def assemble(c):
        @pl.loop(1, TM)
        def _(d):
            turn_copy(c, d).wait_recv()

        for s in range(TM):
            for h in range(2):
                own = recv[c, s, h, frames:, :]
                if s + 1 < TM:
                    ahead = recv[c, s + 1, h, :frames, :]
                    own = (own.astype(jnp.float32) + ahead.astype(jnp.float32)).astype(jnp.bfloat16)
                blocks[c, i, h, s * frames:(s + 1) * frames, :] = own
        for side in range(2):
            y_copy(c, 0, side).start()
        for d in range(1, NZ):
            z_copy(c, d).start()

    def spread(c):
        for d in range(1, NZ):
            z_copy(c, d).wait_recv()
            for side in range(2):
                y_copy(c, d, side).start()

    def forward(c):
        for d in range(NZ):
            for side in range(2):
                y_copy(c, d, side).wait_recv()
                f_copy(c, d, side).start()

    def correlate(c):
        for d in range(NZ):
            for side in range(2):
                f_copy(c, d, side).wait_recv()
        re = blocks[c, i, 0].T
        im = blocks[c, i, 1].T
        span = re.shape[1]
        lt[:width, :span] = re
        lt[:width, span:] = im
        lt[width:, :span] = im
        lt[width:, span:] = -re

        @pl.loop(0, INP // 2)
        def _(q):
            left = blocks[c, 2 * q].reshape(2 * span, width)
            right = blocks[c, 2 * q + 1].reshape(2 * span, width)
            prod = jnp.dot(lt[...], jnp.concatenate([left, right], axis=1), preferred_element_type=jnp.float32)
            prod = (prod * (1.0 / span)).astype(jnp.bfloat16)
            at = pl.ds(pl.multiple_of(q * 2 * width, 2 * width), 2 * width)
            vout[c, 0, :, at] = prod[:width]
            vout[c, 1, :, at] = prod[width:]

        pltpu.make_async_copy(vout.at[c], out_hbm.at[:, c], out_sem.at[c]).start()

    half = pairs // 2
    weights(0)
    filtered(0, 0, pairs)
    finish(0)
    pl.semaphore_wait(barrier, TM - 1 + NZ - 1 + 2)
    turn_start(0)
    for c in range(1, CH_DEV):
        weights(c)
        filtered(c, 0, half)
        assemble(c - 1)
        filtered(c, half, pairs)
        finish(c)
        turn_start(c)
        spread(c - 1)
        if c >= 2:
            forward(c - 2)
    assemble(CH_DEV - 1)
    spread(CH_DEV - 1)
    for c in range(CH_DEV - 2):
        correlate(c)
    forward(CH_DEV - 2)
    forward(CH_DEV - 1)
    correlate(CH_DEV - 2)
    correlate(CH_DEV - 1)
    for c in range(CH_DEV):
        @pl.loop(1, TM)
        def _(d):
            turn_copy(c, d).wait_send()

        for d in range(1, NZ):
            z_copy(c, d).wait_send()
        for d in range(NZ):
            for side in range(2):
                y_copy(c, d, side).wait_send()
                f_copy(c, d, side).wait_send()
        pltpu.make_async_copy(vout.at[c], out_hbm.at[:, c], out_sem.at[c]).wait()


def on_device(samples, filter_taps):
    ntaps, nch = filter_taps.shape
    width = samples.shape[2]
    frames = samples.shape[1] // nch
    total = frames * TM
    rows = 2 * TM
    local = samples.reshape(2, frames, nch, width)
    dma = pltpu.SemaphoreType.DMA
    return pl.pallas_call(
        kernel,
        out_shape=jax.ShapeDtypeStruct((2, CH_DEV, width, INP * width), jnp.bfloat16),
        in_specs=[
            pl.BlockSpec(memory_space=pl.ANY),
            pl.BlockSpec(memory_space=pltpu.VMEM),
            pl.BlockSpec(memory_space=pltpu.VMEM),
        ],
        out_specs=pl.BlockSpec(memory_space=pl.ANY),
        scratch_shapes=[
            pltpu.VMEM((2, frames, nch, width), jnp.bfloat16),
            pltpu.VMEM((ntaps * rows, 2 * nch), jnp.bfloat16),
            pltpu.VMEM((ntaps * rows, 2 * nch), jnp.bfloat16),
            pltpu.VMEM((2 * frames * rows, width), jnp.float32),
            pltpu.VMEM((CH_DEV, TM, 2, 2 * frames, width), jnp.bfloat16),
            pltpu.VMEM((CH_DEV, TM, 2, 2 * frames, width), jnp.bfloat16),
            pltpu.VMEM((CH_DEV, INP, 2, total, width), jnp.bfloat16),
            pltpu.VMEM((2 * width, 2 * total), jnp.bfloat16),
            pltpu.VMEM((CH_DEV, 2, width, INP * width), jnp.bfloat16),
            dma((frames // 2,)),
            dma((CH_DEV, TM)),
            dma((CH_DEV, TM)),
            dma((CH_DEV, NZ)),
            dma((CH_DEV, NZ)),
            dma((CH_DEV, 2, NZ)),
            dma((CH_DEV, 2, NZ)),
            dma((CH_DEV, 2, NZ)),
            dma((CH_DEV, 2, NZ)),
            dma((CH_DEV,)),
        ],
        compiler_params=pltpu.CompilerParams(
            collective_id=0, has_side_effects=True, vmem_limit_bytes=60 * 1024 * 1024),
        name="correlator",
    )(local, filter_taps, jnp.asarray(trig_table(nch)))


def solution(mesh):
    in_specs = (P(None, "tm", "input"), P())
    out_specs = P(None, "tm", "input", None)
    return jax.shard_map(
        on_device, mesh=mesh, in_specs=in_specs, out_specs=out_specs, check_vma=False
    )
```

```python
import functools

import jax
import jax.numpy as jnp
import numpy as np
from jax import lax
from jax.experimental import pallas as pl
from jax.experimental.pallas import tpu as pltpu
from jax.sharding import PartitionSpec as P

MESH = pl.DeviceIdType.MESH
CH_DEV = 4
TM = 16
NY = 4
NZ = 4
INP = NY * NZ
GROUP = 8


def trig_table(nch):
    chan = CH_DEV * np.arange(TM)[None, :] + np.arange(CH_DEV)[:, None]
    phase = chan[:, :, None] * np.arange(nch)[None, None, :] % nch
    theta = 2.0 * np.pi / nch * phase
    scale = 1.0 / np.sqrt(nch)
    return np.stack([np.cos(theta) * scale, np.sin(theta) * scale]).astype(np.float32)


def kernel(x_hbm, taps_ref, trig_ref, out_hbm, xv, ghi, acc, part, recv, mid, ahead, merged, crossed, blocks, lt, vout, vsend, vin,
           x_sem, turn_send, turn_recv, mid_send, mid_recv, ahead_send, ahead_recv, cross_send, cross_recv,
           z_send, z_recv, zf_send, y_send, y_recv, b_send, b_recv, v_send, v_recv, out_sem):
    t = lax.axis_index("tm")
    i = lax.axis_index("input")
    x = t // 4
    zhi = lax.rem(t // 2, 2)
    core = lax.rem(t, 2)
    other = 1 - zhi
    z = i // NY
    y = lax.rem(i, NY)
    q = 2 * x + core
    ring = zhi * NZ + z
    toward = jnp.where(x == 0, 1, -1)
    up = lax.rem(y + 1, NY)
    down = lax.rem(y + NY - 1, NY)
    ntaps, nch = taps_ref.shape
    frames = xv.shape[1]
    width = xv.shape[3]
    rows = 2 * TM
    pairs = frames // 2

    def at_ring(member, place):
        place = lax.rem(place + 2 * NZ, 2 * NZ)
        return {"tm": (member // 2) * 4 + 2 * (place // NZ) + lax.rem(member, 2), "input": lax.rem(place, NZ) * NY + y}

    def at_group(member):
        return at_ring(member, ring)

    def at_z(place):
        return {"tm": t, "input": place * NY + y}

    def at_y(place):
        return {"tm": t, "input": z * NY + place}

    def x_copy(p):
        sl = pl.ds(2 * p, 2)
        return pltpu.make_async_copy(x_hbm.at[:, sl], xv.at[:, sl], x_sem.at[p])

    for p in range(pairs):
        x_copy(p).start()

    barrier = pltpu.get_barrier_semaphore()
    peers = [at_group(lax.rem(q + d, GROUP)) for d in range(1, GROUP)]
    peers += [at_ring(q, ring + step) for step in (3, -3)]
    peers += [at_z(lax.rem(z + d, NZ)) for d in range(1, NZ)]
    peers += [at_y(up), at_y(down)]
    for peer in peers:
        pl.semaphore_signal(barrier, inc=1, device_id=peer, device_id_type=MESH)
    steps = (1, -1, NZ)

    @pl.loop(0, GROUP)
    def _(member):
        for step in steps:
            pl.semaphore_signal(barrier, inc=1, device_id=at_ring(member, ring + step), device_id_type=MESH)

    def weights(c):
        cosine = trig_ref[0, c]
        sine = trig_ref[1, c]

        @pl.loop(0, ntaps)
        def _(tap):
            h = taps_ref[pl.ds(tap, 1), :]
            co = cosine * h
            si = sine * h
            for r0, c0, val in ((0, 0, co), (0, nch, si), (TM, 0, -si), (TM, nch, co)):
                at = pl.multiple_of(tap * rows + r0, TM)
                ghi[pl.ds(at, TM), c0:c0 + nch] = val.astype(jnp.bfloat16)

        acc[...] = jnp.zeros_like(acc)

    def filtered(c, lo, hi):
        @pl.loop(lo, hi)
        def _(p):
            if c == 0:
                x_copy(p).wait()
            b0 = jnp.concatenate([xv[0, 2 * p], xv[0, 2 * p + 1]], axis=1)
            b1 = jnp.concatenate([xv[1, 2 * p], xv[1, 2 * p + 1]], axis=1)
            both = jnp.concatenate([b0, b1], axis=0)
            prod = jnp.dot(ghi[...], both, preferred_element_type=jnp.float32)
            for tap in range(ntaps):
                for j in range(2):
                    at = pl.ds(pl.multiple_of((2 * p + j - tap + frames) * rows, rows), rows)
                    acc[at, :] += prod[tap * rows:(tap + 1) * rows, j * width:(j + 1) * width]

    def turn_copy(c, d):
        member = lax.rem(q + d, GROUP)
        return pltpu.make_async_remote_copy(
            src_ref=part.at[c, member, zhi], dst_ref=recv.at[c, q],
            send_sem=turn_send.at[c, d], recv_sem=turn_recv.at[c, d],
            device_id=at_group(member), device_id_type=MESH)

    def mid_copy(c, d):
        member = lax.rem(q + d, GROUP)
        return pltpu.make_async_remote_copy(
            src_ref=part.at[c, member, other], dst_ref=mid.at[c, q],
            send_sem=mid_send.at[c, d], recv_sem=mid_recv.at[c, d],
            device_id=at_ring(member, ring + toward), device_id_type=MESH)

    def ahead_copy(c, member):
        return pltpu.make_async_remote_copy(
            src_ref=part.at[c, member, other, :, pl.ds(0, frames)], dst_ref=ahead.at[c, x],
            send_sem=ahead_send.at[c, member], recv_sem=ahead_recv.at[c, x],
            device_id=at_ring(member, ring + NZ), device_id_type=MESH)

    def ahead_arrival(c, k):
        return pltpu.make_async_remote_copy(
            src_ref=part.at[c, 0, 0, :, pl.ds(0, frames)], dst_ref=ahead.at[c, k],
            send_sem=ahead_send.at[c, 0], recv_sem=ahead_recv.at[c, k],
            device_id=at_ring(q, ring + NZ), device_id_type=MESH)

    def cross_copy(c, side):
        sl = (pl.ds(0, 1), pl.ds(1, 3))[side]
        return pltpu.make_async_remote_copy(
            src_ref=merged.at[c, sl], dst_ref=crossed.at[c, sl],
            send_sem=cross_send.at[c, side], recv_sem=cross_recv.at[c, side],
            device_id=at_ring(q, ring + (3, -3)[side]), device_id_type=MESH)

    def finish(c):
        for h in range(2):
            for owner in range(TM):
                r = h * TM + owner
                member, side = (owner // 4) * 2 + owner % 2, (owner // 2) % 2
                part[c, member, side, h] = acc[pl.ds(r, rows, stride=rows), :].astype(jnp.bfloat16)
        recv[c, q] = part[c, q, zhi]

        @pl.when(core == 0)
        def _():
            for member in range(GROUP):
                ahead_copy(c, member).start()

        for d in range(GROUP):
            mid_copy(c, d).start()
        for d in range(1, GROUP):
            turn_copy(c, d).start()

    def segments(c, slot, stage):
        return blocks.at[c, slot, pl.ds(2 * stage, 2)]

    def z_copy(c, d, stage):
        ref = segments(c, i, stage)
        return pltpu.make_async_remote_copy(
            src_ref=ref, dst_ref=ref,
            send_sem=z_send.at[c, d, stage], recv_sem=z_recv.at[c, d, stage],
            device_id=at_z(lax.rem(z + d, NZ)), device_id_type=MESH)

    def z_far(d):
        return (z == 3) if d == 1 else (z == 0) if d == 3 else None

    def z_each(d, act):
        far = z_far(d)
        if far is None:
            act()
        else:
            pl.when(jnp.logical_not(far))(act)

    inner = jnp.logical_or(z == 1, z == 2)

    def zf_copy(c, stage):
        source = lax.rem(z + 2, NZ)
        target = jnp.where(z == 1, 0, 3)
        ref = segments(c, source * NY + y, stage)
        return pltpu.make_async_remote_copy(
            src_ref=ref, dst_ref=ref,
            send_sem=zf_send.at[c, stage], recv_sem=z_recv.at[c, jnp.where(z == 1, 1, 3), stage],
            device_id=at_z(target), device_id_type=MESH)

    def fwd(c):
        return (up, down)[c % 2]

    def back(c):
        return (down, up)[c % 2]

    def y_copy(c, d, stage):
        ref = segments(c, lax.rem(z + NZ - d, NZ) * NY + y, stage)
        return pltpu.make_async_remote_copy(
            src_ref=ref, dst_ref=ref,
            send_sem=y_send.at[c, d, stage], recv_sem=y_recv.at[c, d, stage],
            device_id=at_y(fwd(c)), device_id_type=MESH)

    def b_copy(c, stage):
        ref = segments(c, i, stage)
        return pltpu.make_async_remote_copy(
            src_ref=ref, dst_ref=ref,
            send_sem=b_send.at[c, stage], recv_sem=b_recv.at[c, stage],
            device_id=at_y(back(c)), device_id_type=MESH)

    def v_copy(c, side):
        return pltpu.make_async_remote_copy(
            src_ref=vsend.at[c, side], dst_ref=vin.at[c, side],
            send_sem=v_send.at[c, side], recv_sem=v_recv.at[c, side],
            device_id=at_y((back(c), fwd(c))[side]), device_id_type=MESH)

    def total(a, b):
        return (a.astype(jnp.float32) + b.astype(jnp.float32)).astype(jnp.bfloat16)

    def send_own(c, stage):
        y_copy(c, 0, stage).start()
        b_copy(c, stage).start()
        for d in (2, 1, 3):
            z_each(d, lambda: z_copy(c, d, stage).start())

    def first_half(c):
        for d in range(GROUP):
            mid_copy(c, d).wait_recv()
        for k in range(4):
            for h in range(2):
                merged[c, k, 0, h] = total(mid[c, 2 * k, h, frames:, :], mid[c, 2 * k + 1, h, :frames, :])
                merged[c, k, 1, h] = mid[c, 2 * k + 1, h, frames:, :]
        for side in range(2):
            cross_copy(c, side).start()
        for d in range(1, GROUP):
            turn_copy(c, d).wait_recv()
        for k in range(4):
            ahead_arrival(c, k).wait_recv()
        for k in range(4):
            there = jnp.minimum(k + zhi, 3)
            for h in range(2):
                at = slice(k * frames, (k + 1) * frames)
                blocks[c, i, 0, h, at] = total(recv[c, 2 * k, h, frames:, :], recv[c, 2 * k + 1, h, :frames, :])
                rest = ahead[c, there, h].astype(jnp.float32)
                if k == 3:
                    rest = jnp.where(zhi == 0, rest, 0.0)
                blocks[c, i, 1, h, at] = total(recv[c, 2 * k + 1, h, frames:, :], rest)
        send_own(c, 0)

    def second_half(c):
        for side in range(2):
            cross_copy(c, side).wait_recv()
        for k in range(4):
            here = jnp.minimum(k + other, 3)
            for h in range(2):
                at = slice(k * frames, (k + 1) * frames)
                blocks[c, i, 2, h, at] = crossed[c, k, 0, h]
                rest = recv[c, 2 * here, h, :frames, :].astype(jnp.float32)
                if k == 3:
                    rest = jnp.where(zhi == 1, rest, 0.0)
                blocks[c, i, 3, h, at] = total(crossed[c, k, 1, h], rest)
        send_own(c, 1)

    def spread(c, stage):
        for d in (2, 1, 3):
            z_copy(c, d, stage).wait_recv()
            if d == 2:
                pl.when(inner)(lambda: zf_copy(c, stage).start())
            y_copy(c, d, stage).start()

    def left_rows(c, slot):
        span = 2 * blocks.shape[4]
        for seg in range(4):
            re = blocks[c, slot, seg, 0]
            im = blocks[c, slot, seg, 1]
            lt[:width, seg * span:(seg + 1) * span] = jnp.concatenate([re, im], axis=0).T
            lt[width:, seg * span:(seg + 1) * span] = jnp.concatenate([im, -re], axis=0).T

    def products(c, column, put):
        depth = 8 * blocks.shape[4]
        for n in range(0, NZ, 2):
            pair = [blocks[c, (n + k) * NY + column].reshape(depth, width) for k in range(2)]
            prod = jnp.dot(lt[...], jnp.concatenate(pair, axis=1), preferred_element_type=jnp.float32)
            prod = (prod * (2.0 / depth)).astype(jnp.bfloat16)
            for k in range(2):
                for h in range(2):
                    put(n + k, h, prod[h * width:(h + 1) * width, k * width:(k + 1) * width])

    def put_row(c, column):
        def put(n, h, value):
            at = pl.ds(pl.multiple_of((n * NY + column) * width, width), width)
            vout[c, h, :, at] = value
        return put

    def put_send(c, side):
        def put(n, h, value):
            vsend[c, side, n, h] = value
        return put

    def arrived(c):
        for d in (0, 2, 1, 3):
            for stage in range(2):
                y_copy(c, d, stage).wait_recv()
        for stage in range(2):
            b_copy(c, stage).wait_recv()

    def correlate(c):
        arrived(c)
        left_rows(c, z * NY + back(c))
        products(c, y, put_send(c, 0))
        v_copy(c, 0).start()
        left_rows(c, z * NY + fwd(c))
        products(c, back(c), put_send(c, 1))
        v_copy(c, 1).start()
        left_rows(c, i)
        for column in (y, back(c)):
            products(c, column, put_row(c, column))

    def collect(c):
        for side in range(2):
            v_copy(c, side).wait_recv()
            column = (fwd(c), lax.rem(y + 2, NY))[side]
            for n in range(NZ):
                for h in range(2):
                    put_row(c, column)(n, h, vin[c, side, n, h])
        pltpu.make_async_copy(vout.at[c], out_hbm.at[:, c], out_sem.at[c]).start()

    def channel(c):
        weights(c)
        filtered(c, 0, pairs)
        if c == 0:
            pl.semaphore_wait(barrier, len(peers) + GROUP * len(steps))
        finish(c)

    channel(0)
    channel(1)
    first_half(0)
    channel(2)
    second_half(0)
    spread(0, 0)
    first_half(1)
    channel(3)
    spread(0, 1)
    second_half(1)
    spread(1, 0)
    first_half(2)
    spread(1, 1)
    second_half(2)
    spread(2, 0)
    first_half(3)
    correlate(0)
    spread(2, 1)
    second_half(3)
    spread(3, 0)
    correlate(1)
    spread(3, 1)
    collect(0)
    correlate(2)
    collect(1)
    correlate(3)
    collect(2)
    collect(3)
    for c in range(CH_DEV):
        for d in range(1, GROUP):
            turn_copy(c, d).wait_send()
        for d in range(GROUP):
            mid_copy(c, d).wait_send()

        @pl.when(core == 0)
        def _():
            for member in range(GROUP):
                ahead_copy(c, member).wait_send()

        for side in range(2):
            cross_copy(c, side).wait_send()
        for stage in range(2):
            for d in range(1, NZ):
                z_each(d, lambda: z_copy(c, d, stage).wait_send())
            pl.when(inner)(lambda: zf_copy(c, stage).wait_send())
            b_copy(c, stage).wait_send()
            for d in range(NZ):
                y_copy(c, d, stage).wait_send()
        for side in range(2):
            v_copy(c, side).wait_send()
        pltpu.make_async_copy(vout.at[c], out_hbm.at[:, c], out_sem.at[c]).wait()


def on_device(samples, filter_taps):
    ntaps, nch = filter_taps.shape
    width = samples.shape[2]
    frames = samples.shape[1] // nch
    total = frames * TM
    rows = 2 * TM
    local = samples.reshape(2, frames, nch, width)
    dma = pltpu.SemaphoreType.DMA
    return pl.pallas_call(
        kernel,
        out_shape=jax.ShapeDtypeStruct((2, CH_DEV, width, INP * width), jnp.bfloat16),
        in_specs=[
            pl.BlockSpec(memory_space=pltpu.HBM),
            pl.BlockSpec(memory_space=pltpu.VMEM),
            pl.BlockSpec(memory_space=pltpu.VMEM),
        ],
        out_specs=pl.BlockSpec(memory_space=pl.ANY),
        scratch_shapes=[
            pltpu.VMEM((2, frames, nch, width), jnp.bfloat16),
            pltpu.VMEM((ntaps * rows, 2 * nch), jnp.bfloat16),
            pltpu.VMEM((2 * frames * rows, width), jnp.float32),
            pltpu.VMEM((CH_DEV, GROUP, 2, 2, 2 * frames, width), jnp.bfloat16),
            pltpu.VMEM((CH_DEV, GROUP, 2, 2 * frames, width), jnp.bfloat16),
            pltpu.VMEM((CH_DEV, GROUP, 2, 2 * frames, width), jnp.bfloat16),
            pltpu.VMEM((CH_DEV, 4, 2, frames, width), jnp.bfloat16),
            pltpu.VMEM((CH_DEV, 4, 2, 2, frames, width), jnp.bfloat16),
            pltpu.VMEM((CH_DEV, 4, 2, 2, frames, width), jnp.bfloat16),
            pltpu.VMEM((CH_DEV, INP, 4, 2, total // 4, width), jnp.bfloat16),
            pltpu.VMEM((2 * width, 2 * total), jnp.bfloat16),
            pltpu.VMEM((CH_DEV, 2, width, INP * width), jnp.bfloat16),
            pltpu.VMEM((CH_DEV, 2, NZ, 2, width, width), jnp.bfloat16),
            pltpu.VMEM((CH_DEV, 2, NZ, 2, width, width), jnp.bfloat16),
            dma((frames // 2,)),
            dma((CH_DEV, GROUP)),
            dma((CH_DEV, GROUP)),
            dma((CH_DEV, GROUP)),
            dma((CH_DEV, GROUP)),
            dma((CH_DEV, GROUP)),
            dma((CH_DEV, 4)),
            dma((CH_DEV, 2)),
            dma((CH_DEV, 2)),
            dma((CH_DEV, NZ, 2)),
            dma((CH_DEV, NZ, 2)),
            dma((CH_DEV, 2)),
            dma((CH_DEV, NZ, 2)),
            dma((CH_DEV, NZ, 2)),
            dma((CH_DEV, 2)),
            dma((CH_DEV, 2)),
            dma((CH_DEV, 2)),
            dma((CH_DEV, 2)),
            dma((CH_DEV,)),
        ],
        compiler_params=pltpu.CompilerParams(
            collective_id=0, has_side_effects=True, vmem_limit_bytes=54 * 1024 * 1024),
        name="correlator",
    )(local, filter_taps, jnp.asarray(trig_table(nch)))


def solution(mesh):
    in_specs = (P(None, "tm", "input"), P())
    out_specs = P(None, "tm", "input", None)
    return jax.shard_map(
        on_device, mesh=mesh, in_specs=in_specs, out_specs=out_specs, check_vma=False
    )
```

```python
import functools

import jax
import jax.numpy as jnp
import numpy as np
from jax import lax
from jax.experimental import pallas as pl
from jax.experimental.pallas import tpu as pltpu
from jax.sharding import PartitionSpec as P

MESH = pl.DeviceIdType.MESH
CH_DEV = 4
TM = 16
NY = 4
NZ = 4
INP = NY * NZ
GROUP = 8


def trig_table(nch):
    chan = CH_DEV * np.arange(TM)[None, :] + np.arange(CH_DEV)[:, None]
    phase = chan[:, :, None] * np.arange(nch)[None, None, :] % nch
    theta = 2.0 * np.pi / nch * phase
    scale = 1.0 / np.sqrt(nch)
    return np.stack([np.cos(theta) * scale, np.sin(theta) * scale]).astype(np.float32)


def kernel(x_hbm, taps_ref, trig_ref, out_hbm, xv, ghi, acc, part, recv, ahead, far, blocks, lt, vout, vsend, vin,
           x_sem, turn_send, turn_recv, ahead_send, ahead_recv,
           z_send, z_recv, g_send, g_recv, t_send, y_send, y_recv, b_send, b_recv, v_send, v_recv, out_sem):
    t = lax.axis_index("tm")
    i = lax.axis_index("input")
    x = t // 4
    zhi = lax.rem(t // 2, 2)
    core = lax.rem(t, 2)
    other = 1 - zhi
    z = i // NY
    y = lax.rem(i, NY)
    q = 2 * x + core
    ring = zhi * NZ + z
    up = lax.rem(y + 1, NY)
    down = lax.rem(y + NY - 1, NY)
    ntaps, nch = taps_ref.shape
    frames = xv.shape[1]
    width = xv.shape[3]
    rows = 2 * TM
    pairs = frames // 2

    def at_ring(member, place):
        place = lax.rem(place + 2 * NZ, 2 * NZ)
        return {"tm": (member // 2) * 4 + 2 * (place // NZ) + lax.rem(member, 2), "input": lax.rem(place, NZ) * NY + y}

    def at_group(member):
        return at_ring(member, ring)

    def at_z(place):
        return {"tm": t, "input": place * NY + y}

    def at_y(place):
        return {"tm": t, "input": z * NY + place}

    def x_copy(p):
        sl = pl.ds(2 * p, 2)
        return pltpu.make_async_copy(x_hbm.at[:, sl], xv.at[:, sl], x_sem.at[p])

    for p in range(pairs):
        x_copy(p).start()

    barrier = pltpu.get_barrier_semaphore()
    peers = [at_group(lax.rem(q + d, GROUP)) for d in range(1, GROUP)]
    peers += [at_ring(q, other * NZ + lax.rem(z + d, NZ)) for d in range(1, NZ)]
    peers += [at_z(lax.rem(z + d, NZ)) for d in range(1, NZ)]
    peers += [at_y(up), at_y(down)]
    for peer in peers:
        pl.semaphore_signal(barrier, inc=1, device_id=peer, device_id_type=MESH)

    @pl.loop(0, GROUP)
    def _(member):
        pl.semaphore_signal(barrier, inc=1, device_id=at_ring(member, ring + NZ), device_id_type=MESH)

    def weights(c):
        cosine = trig_ref[0, c]
        sine = trig_ref[1, c]

        @pl.loop(0, ntaps)
        def _(tap):
            h = taps_ref[pl.ds(tap, 1), :]
            co = cosine * h
            si = sine * h
            for r0, c0, val in ((0, 0, co), (0, nch, si), (TM, 0, -si), (TM, nch, co)):
                at = pl.multiple_of(tap * rows + r0, TM)
                ghi[pl.ds(at, TM), c0:c0 + nch] = val.astype(jnp.bfloat16)

        acc[...] = jnp.zeros_like(acc)

    def filtered(c, lo, hi):
        @pl.loop(lo, hi)
        def _(p):
            if c == 0:
                x_copy(p).wait()
            b0 = jnp.concatenate([xv[0, 2 * p], xv[0, 2 * p + 1]], axis=1)
            b1 = jnp.concatenate([xv[1, 2 * p], xv[1, 2 * p + 1]], axis=1)
            both = jnp.concatenate([b0, b1], axis=0)
            prod = jnp.dot(ghi[...], both, preferred_element_type=jnp.float32)
            for tap in range(ntaps):
                for j in range(2):
                    at = pl.ds(pl.multiple_of((2 * p + j - tap + frames) * rows, rows), rows)
                    acc[at, :] += prod[tap * rows:(tap + 1) * rows, j * width:(j + 1) * width]

    def turn_copy(c, d):
        member = lax.rem(q + d, GROUP)
        return pltpu.make_async_remote_copy(
            src_ref=part.at[c, member], dst_ref=recv.at[c, q],
            send_sem=turn_send.at[c, d], recv_sem=turn_recv.at[c, d],
            device_id=at_group(member), device_id_type=MESH)

    def ahead_copy(c, member):
        return pltpu.make_async_remote_copy(
            src_ref=part.at[c, member, :, :, pl.ds(0, frames)], dst_ref=ahead.at[c, x],
            send_sem=ahead_send.at[c, member], recv_sem=ahead_recv.at[c, x],
            device_id=at_ring(member, ring + NZ), device_id_type=MESH)

    def ahead_arrival(c, k):
        return pltpu.make_async_remote_copy(
            src_ref=part.at[c, 0, :, :, pl.ds(0, frames)], dst_ref=ahead.at[c, k],
            send_sem=ahead_send.at[c, 0], recv_sem=ahead_recv.at[c, k],
            device_id=at_ring(q, ring + NZ), device_id_type=MESH)

    def finish(c):
        for h in range(2):
            for owner in range(TM):
                r = h * TM + owner
                member, side = (owner // 4) * 2 + owner % 2, (owner // 2) % 2
                part[c, member, side, h] = acc[pl.ds(r, rows, stride=rows), :].astype(jnp.bfloat16)
        recv[c, q] = part[c, q]

        @pl.when(core == 0)
        def _():
            for member in range(GROUP):
                ahead_copy(c, member).start()

        for d in range(1, GROUP):
            turn_copy(c, d).start()

    def segments(c, slot, group):
        return blocks.at[c, slot, pl.ds(2 * group, 2)]

    def near_copy(c, d):
        ref = segments(c, i, zhi)
        return pltpu.make_async_remote_copy(
            src_ref=ref, dst_ref=ref,
            send_sem=z_send.at[c, d], recv_sem=z_recv.at[c, d],
            device_id=at_z(lax.rem(z + d, NZ)), device_id_type=MESH)

    def far_copy(c, d):
        return pltpu.make_async_remote_copy(
            src_ref=far.at[c], dst_ref=segments(c, i, zhi),
            send_sem=g_send.at[c, d], recv_sem=g_recv.at[c, z],
            device_id=at_ring(q, other * NZ + lax.rem(z + d, NZ)), device_id_type=MESH)

    def far_arrival(c, source):
        ref = segments(c, source * NY + y, other)
        return pltpu.make_async_remote_copy(
            src_ref=ref, dst_ref=ref,
            send_sem=g_send.at[c, 0], recv_sem=g_recv.at[c, source],
            device_id=at_z(lax.rem(z + 1, NZ)), device_id_type=MESH)

    def tie_copy(c, source, slot):
        ref = segments(c, source * NY + y, other)
        return pltpu.make_async_remote_copy(
            src_ref=ref, dst_ref=ref,
            send_sem=t_send.at[c, slot], recv_sem=g_recv.at[c, source],
            device_id=at_z(source), device_id_type=MESH)

    def fwd(c):
        return (up, down)[c % 2]

    def back(c):
        return (down, up)[c % 2]

    def y_copy(c, d, stage):
        ref = segments(c, lax.rem(z + NZ - d, NZ) * NY + y, (zhi, other)[stage])
        return pltpu.make_async_remote_copy(
            src_ref=ref, dst_ref=ref,
            send_sem=y_send.at[c, d, stage], recv_sem=y_recv.at[c, d, stage],
            device_id=at_y(fwd(c)), device_id_type=MESH)

    def b_copy(c, stage):
        ref = segments(c, i, (zhi, other)[stage])
        return pltpu.make_async_remote_copy(
            src_ref=ref, dst_ref=ref,
            send_sem=b_send.at[c, stage], recv_sem=b_recv.at[c, stage],
            device_id=at_y(back(c)), device_id_type=MESH)

    def v_copy(c, side):
        return pltpu.make_async_remote_copy(
            src_ref=vsend.at[c, side], dst_ref=vin.at[c, side],
            send_sem=v_send.at[c, side], recv_sem=v_recv.at[c, side],
            device_id=at_y((back(c), fwd(c))[side]), device_id_type=MESH)

    def total(a, b):
        return (a.astype(jnp.float32) + b.astype(jnp.float32)).astype(jnp.bfloat16)

    def merge(c):
        for d in range(1, GROUP):
            turn_copy(c, d).wait_recv()
        for k in range(4):
            ahead_arrival(c, k).wait_recv()
        for group in (other, zhi):
            for k in range(4):
                there = jnp.minimum(k + zhi, 3)
                at = slice(k * frames, (k + 1) * frames)
                for h in range(2):
                    first = total(recv[c, 2 * k, group, h, frames:, :], recv[c, 2 * k + 1, group, h, :frames, :])
                    rest = ahead[c, there, group, h].astype(jnp.float32)
                    if k == 3:
                        rest = jnp.where(zhi == 0, rest, 0.0)
                    second = total(recv[c, 2 * k + 1, group, h, frames:, :], rest)
                    if group is other:
                        far[c, 0, h, at] = first
                        far[c, 1, h, at] = second
                    else:
                        blocks[c, i, 2 * zhi, h, at] = first
                        blocks[c, i, 2 * zhi + 1, h, at] = second
            if group is other:
                for d in (1, 3, 2):
                    far_copy(c, d).start()
        y_copy(c, 0, 0).start()
        b_copy(c, 0).start()
        for d in (2, 1, 3):
            near_copy(c, d).start()

    def spread_near(c):
        for d in (2, 1, 3):
            near_copy(c, d).wait_recv()
            y_copy(c, d, 0).start()

    def spread_far(c):
        for d in (1, 3, 2):
            source = lax.rem(z + NZ - d, NZ)
            far_arrival(c, source).wait_recv()
            if d == 1:
                pl.when(z >= 1)(lambda: tie_copy(c, z - 1, 0).start())
            if d == 3:
                pl.when(z == 2)(lambda: tie_copy(c, 3, 1).start())
            y_copy(c, d, 1).start()

    def spread_tie(c):
        far_arrival(c, z).wait_recv()
        y_copy(c, 0, 1).start()
        b_copy(c, 1).start()

    def left_rows(c, slot):
        span = 2 * blocks.shape[4]
        for seg in range(4):
            re = blocks[c, slot, seg, 0]
            im = blocks[c, slot, seg, 1]
            lt[:width, seg * span:(seg + 1) * span] = jnp.concatenate([re, im], axis=0).T
            lt[width:, seg * span:(seg + 1) * span] = jnp.concatenate([im, -re], axis=0).T

    def products(c, column, put):
        depth = 8 * blocks.shape[4]
        for n in range(0, NZ, 2):
            pair = [blocks[c, (n + k) * NY + column].reshape(depth, width) for k in range(2)]
            prod = jnp.dot(lt[...], jnp.concatenate(pair, axis=1), preferred_element_type=jnp.float32)
            prod = (prod * (2.0 / depth)).astype(jnp.bfloat16)
            for k in range(2):
                for h in range(2):
                    put(n + k, h, prod[h * width:(h + 1) * width, k * width:(k + 1) * width])

    def put_row(c, column):
        def put(n, h, value):
            at = pl.ds(pl.multiple_of((n * NY + column) * width, width), width)
            vout[c, h, :, at] = value
        return put

    def put_send(c, side):
        def put(n, h, value):
            vsend[c, side, n, h] = value
        return put

    def arrived(c):
        for d in (0, 2, 1, 3):
            for stage in range(2):
                y_copy(c, d, stage).wait_recv()
        for stage in range(2):
            b_copy(c, stage).wait_recv()

    def correlate(c):
        arrived(c)
        left_rows(c, z * NY + back(c))
        products(c, y, put_send(c, 0))
        v_copy(c, 0).start()
        left_rows(c, z * NY + fwd(c))
        products(c, back(c), put_send(c, 1))
        v_copy(c, 1).start()
        left_rows(c, i)
        for column in (y, back(c)):
            products(c, column, put_row(c, column))

    def collect(c):
        for side in range(2):
            v_copy(c, side).wait_recv()
            column = (fwd(c), lax.rem(y + 2, NY))[side]
            for n in range(NZ):
                for h in range(2):
                    put_row(c, column)(n, h, vin[c, side, n, h])
        pltpu.make_async_copy(vout.at[c], out_hbm.at[:, c], out_sem.at[c]).start()

    def channel(c):
        weights(c)
        filtered(c, 0, pairs)
        if c == 0:
            pl.semaphore_wait(barrier, len(peers) + GROUP)
        finish(c)

    channel(0)
    channel(1)
    merge(0)
    channel(2)
    spread_near(0)
    spread_far(0)
    merge(1)
    channel(3)
    spread_tie(0)
    spread_near(1)
    spread_far(1)
    merge(2)
    spread_tie(1)
    correlate(0)
    spread_near(2)
    spread_far(2)
    merge(3)
    spread_tie(2)
    correlate(1)
    spread_near(3)
    spread_far(3)
    spread_tie(3)
    collect(0)
    correlate(2)
    collect(1)
    correlate(3)
    collect(2)
    collect(3)
    for c in range(CH_DEV):
        for d in range(1, GROUP):
            turn_copy(c, d).wait_send()

        @pl.when(core == 0)
        def _():
            for member in range(GROUP):
                ahead_copy(c, member).wait_send()

        for d in range(1, NZ):
            near_copy(c, d).wait_send()
            far_copy(c, d).wait_send()
        pl.when(z >= 1)(lambda: tie_copy(c, z - 1, 0).wait_send())
        pl.when(z == 2)(lambda: tie_copy(c, 3, 1).wait_send())
        for stage in range(2):
            b_copy(c, stage).wait_send()
            for d in range(NZ):
                y_copy(c, d, stage).wait_send()
        for side in range(2):
            v_copy(c, side).wait_send()
        pltpu.make_async_copy(vout.at[c], out_hbm.at[:, c], out_sem.at[c]).wait()


def on_device(samples, filter_taps):
    ntaps, nch = filter_taps.shape
    width = samples.shape[2]
    frames = samples.shape[1] // nch
    total = frames * TM
    rows = 2 * TM
    local = samples.reshape(2, frames, nch, width)
    dma = pltpu.SemaphoreType.DMA
    return pl.pallas_call(
        kernel,
        out_shape=jax.ShapeDtypeStruct((2, CH_DEV, width, INP * width), jnp.bfloat16),
        in_specs=[
            pl.BlockSpec(memory_space=pltpu.HBM),
            pl.BlockSpec(memory_space=pltpu.VMEM),
            pl.BlockSpec(memory_space=pltpu.VMEM),
        ],
        out_specs=pl.BlockSpec(memory_space=pl.ANY),
        scratch_shapes=[
            pltpu.VMEM((2, frames, nch, width), jnp.bfloat16),
            pltpu.VMEM((ntaps * rows, 2 * nch), jnp.bfloat16),
            pltpu.VMEM((2 * frames * rows, width), jnp.float32),
            pltpu.VMEM((CH_DEV, GROUP, 2, 2, 2 * frames, width), jnp.bfloat16),
            pltpu.VMEM((CH_DEV, GROUP, 2, 2, 2 * frames, width), jnp.bfloat16),
            pltpu.VMEM((CH_DEV, 4, 2, 2, frames, width), jnp.bfloat16),
            pltpu.VMEM((CH_DEV, 2, 2, total // 4, width), jnp.bfloat16),
            pltpu.VMEM((CH_DEV, INP, 4, 2, total // 4, width), jnp.bfloat16),
            pltpu.VMEM((2 * width, 2 * total), jnp.bfloat16),
            pltpu.VMEM((CH_DEV, 2, width, INP * width), jnp.bfloat16),
            pltpu.VMEM((CH_DEV, 2, NZ, 2, width, width), jnp.bfloat16),
            pltpu.VMEM((CH_DEV, 2, NZ, 2, width, width), jnp.bfloat16),
            dma((frames // 2,)),
            dma((CH_DEV, GROUP)),
            dma((CH_DEV, GROUP)),
            dma((CH_DEV, GROUP)),
            dma((CH_DEV, 4)),
            dma((CH_DEV, NZ)),
            dma((CH_DEV, NZ)),
            dma((CH_DEV, NZ)),
            dma((CH_DEV, NZ)),
            dma((CH_DEV, 2)),
            dma((CH_DEV, NZ, 2)),
            dma((CH_DEV, NZ, 2)),
            dma((CH_DEV, 2)),
            dma((CH_DEV, 2)),
            dma((CH_DEV, 2)),
            dma((CH_DEV, 2)),
            dma((CH_DEV,)),
        ],
        compiler_params=pltpu.CompilerParams(
            collective_id=0, has_side_effects=True, vmem_limit_bytes=48 * 1024 * 1024),
        name="correlator",
    )(local, filter_taps, jnp.asarray(trig_table(nch)))


def solution(mesh):
    in_specs = (P(None, "tm", "input"), P())
    out_specs = P(None, "tm", "input", None)
    return jax.shard_map(
        on_device, mesh=mesh, in_specs=in_specs, out_specs=out_specs, check_vma=False
    )
```

```python
import functools

import jax
import jax.numpy as jnp
import numpy as np
from jax import lax
from jax.experimental import pallas as pl
from jax.experimental.pallas import tpu as pltpu
from jax.sharding import PartitionSpec as P

MESH = pl.DeviceIdType.MESH
CH_DEV = 4
TM = 16
NY = 4
NZ = 4
INP = NY * NZ
FWD = (0, 1, 3)
BACK = (0, 2)
GROUP = 8


def trig_table(nch):
    chan = CH_DEV * np.arange(TM)[None, :] + np.arange(CH_DEV)[:, None]
    phase = chan[:, :, None] * np.arange(nch)[None, None, :] % nch
    theta = 2.0 * np.pi / nch * phase
    scale = 1.0 / np.sqrt(nch)
    return np.stack([np.cos(theta) * scale, np.sin(theta) * scale]).astype(np.float32)


def kernel(x_hbm, taps_ref, trig_ref, out_hbm, xv, ghi, acc, part, recv, ahead, far, blocks, lt, vout, vsend, vin,
           x_sem, turn_send, turn_recv, ahead_send, ahead_recv,
           z_send, z_recv, g_send, g_recv, t_send, y_send, y_recv, b_send, b_recv, v_send, v_recv, out_sem):
    t = lax.axis_index("tm")
    i = lax.axis_index("input")
    x = t // 4
    zhi = lax.rem(t // 2, 2)
    core = lax.rem(t, 2)
    other = 1 - zhi
    z = i // NY
    y = lax.rem(i, NY)
    q = 2 * x + core
    ring = zhi * NZ + z
    up = lax.rem(y + 1, NY)
    down = lax.rem(y + NY - 1, NY)
    ntaps, nch = taps_ref.shape
    frames = xv.shape[1]
    width = xv.shape[3]
    rows = 2 * TM
    pairs = frames // 2

    def at_ring(member, place):
        place = lax.rem(place + 2 * NZ, 2 * NZ)
        return {"tm": (member // 2) * 4 + 2 * (place // NZ) + lax.rem(member, 2), "input": lax.rem(place, NZ) * NY + y}

    def at_group(member):
        return at_ring(member, ring)

    def at_z(place):
        return {"tm": t, "input": place * NY + y}

    def at_y(place):
        return {"tm": t, "input": z * NY + place}

    def x_copy(p):
        sl = pl.ds(2 * p, 2)
        return pltpu.make_async_copy(x_hbm.at[:, sl], xv.at[:, sl], x_sem.at[p])

    for p in range(pairs):
        x_copy(p).start()

    barrier = pltpu.get_barrier_semaphore()
    peers = [at_group(lax.rem(q + d, GROUP)) for d in range(1, GROUP)]
    peers += [at_ring(q, other * NZ + lax.rem(z + d, NZ)) for d in range(1, NZ)]
    peers += [at_z(lax.rem(z + d, NZ)) for d in range(1, NZ)]
    peers += [at_y(up), at_y(down)]
    for peer in peers:
        pl.semaphore_signal(barrier, inc=1, device_id=peer, device_id_type=MESH)

    @pl.loop(0, GROUP)
    def _(member):
        pl.semaphore_signal(barrier, inc=1, device_id=at_ring(member, ring + NZ), device_id_type=MESH)

    def weights(c):
        cosine = trig_ref[0, c]
        sine = trig_ref[1, c]

        @pl.loop(0, ntaps)
        def _(tap):
            h = taps_ref[pl.ds(tap, 1), :]
            co = cosine * h
            si = sine * h
            for r0, c0, val in ((0, 0, co), (0, nch, si), (TM, 0, -si), (TM, nch, co)):
                at = pl.multiple_of(tap * rows + r0, TM)
                ghi[pl.ds(at, TM), c0:c0 + nch] = val.astype(jnp.bfloat16)

        acc[...] = jnp.zeros_like(acc)

    def filtered(c, lo, hi):
        @pl.loop(lo, hi)
        def _(p):
            if c == 0:
                x_copy(p).wait()
            b0 = jnp.concatenate([xv[0, 2 * p], xv[0, 2 * p + 1]], axis=1)
            b1 = jnp.concatenate([xv[1, 2 * p], xv[1, 2 * p + 1]], axis=1)
            both = jnp.concatenate([b0, b1], axis=0)
            prod = jnp.dot(ghi[...], both, preferred_element_type=jnp.float32)
            for tap in range(ntaps):
                for j in range(2):
                    at = pl.ds(pl.multiple_of((2 * p + j - tap + frames) * rows, rows), rows)
                    acc[at, :] += prod[tap * rows:(tap + 1) * rows, j * width:(j + 1) * width]

    def turn_copy(c, d):
        member = lax.rem(q + d, GROUP)
        return pltpu.make_async_remote_copy(
            src_ref=part.at[c, member], dst_ref=recv.at[c, q],
            send_sem=turn_send.at[c, d], recv_sem=turn_recv.at[c, d],
            device_id=at_group(member), device_id_type=MESH)

    def ahead_copy(c, member):
        return pltpu.make_async_remote_copy(
            src_ref=part.at[c, member, :, :, pl.ds(0, frames)], dst_ref=ahead.at[c, x],
            send_sem=ahead_send.at[c, member], recv_sem=ahead_recv.at[c, x],
            device_id=at_ring(member, ring + NZ), device_id_type=MESH)

    def ahead_arrival(c, k):
        return pltpu.make_async_remote_copy(
            src_ref=part.at[c, 0, :, :, pl.ds(0, frames)], dst_ref=ahead.at[c, k],
            send_sem=ahead_send.at[c, 0], recv_sem=ahead_recv.at[c, k],
            device_id=at_ring(q, ring + NZ), device_id_type=MESH)

    def finish(c):
        for h in range(2):
            for owner in range(TM):
                r = h * TM + owner
                member, side = (owner // 4) * 2 + owner % 2, (owner // 2) % 2
                part[c, member, side, h] = acc[pl.ds(r, rows, stride=rows), :].astype(jnp.bfloat16)
        recv[c, q] = part[c, q]

        @pl.when(core == 0)
        def _():
            for member in range(GROUP):
                ahead_copy(c, member).start()

        for d in range(1, GROUP):
            turn_copy(c, d).start()

    def segments(c, slot, group):
        return blocks.at[c, slot, pl.ds(2 * group, 2)]

    def near_copy(c, d):
        ref = segments(c, i, zhi)
        return pltpu.make_async_remote_copy(
            src_ref=ref, dst_ref=ref,
            send_sem=z_send.at[c, d], recv_sem=z_recv.at[c, d],
            device_id=at_z(lax.rem(z + d, NZ)), device_id_type=MESH)

    def far_copy(c, d):
        return pltpu.make_async_remote_copy(
            src_ref=far.at[c], dst_ref=segments(c, i, zhi),
            send_sem=g_send.at[c, d], recv_sem=g_recv.at[c, z],
            device_id=at_ring(q, other * NZ + lax.rem(z + d, NZ)), device_id_type=MESH)

    def far_arrival(c, source):
        ref = segments(c, source * NY + y, other)
        return pltpu.make_async_remote_copy(
            src_ref=ref, dst_ref=ref,
            send_sem=g_send.at[c, 0], recv_sem=g_recv.at[c, source],
            device_id=at_z(lax.rem(z + 1, NZ)), device_id_type=MESH)

    def tie_copy(c, source, slot):
        ref = segments(c, source * NY + y, other)
        return pltpu.make_async_remote_copy(
            src_ref=ref, dst_ref=ref,
            send_sem=t_send.at[c, slot], recv_sem=g_recv.at[c, source],
            device_id=at_z(source), device_id_type=MESH)

    def fwd(c):
        return (up, down)[c % 2]

    def back(c):
        return (down, up)[c % 2]

    def y_copy(c, d, stage):
        ref = segments(c, lax.rem(z + NZ - d, NZ) * NY + y, (zhi, other)[stage])
        return pltpu.make_async_remote_copy(
            src_ref=ref, dst_ref=ref,
            send_sem=y_send.at[c, d, stage], recv_sem=y_recv.at[c, d, stage],
            device_id=at_y(fwd(c)), device_id_type=MESH)

    def b_copy(c, d, stage):
        ref = segments(c, lax.rem(z + NZ - d, NZ) * NY + y, (zhi, other)[stage])
        return pltpu.make_async_remote_copy(
            src_ref=ref, dst_ref=ref,
            send_sem=b_send.at[c, d, stage], recv_sem=b_recv.at[c, d, stage],
            device_id=at_y(back(c)), device_id_type=MESH)

    def ring_start(c, d, stage):
        if d in FWD:
            y_copy(c, d, stage).start()
        if d in BACK:
            b_copy(c, d, stage).start()

    def v_copy(c, side):
        sl = pl.ds(0, (4, 3)[side])
        return pltpu.make_async_remote_copy(
            src_ref=vsend.at[c, side, sl], dst_ref=vin.at[c, side, sl],
            send_sem=v_send.at[c, side], recv_sem=v_recv.at[c, side],
            device_id=at_y((back(c), fwd(c))[side]), device_id_type=MESH)

    def total(a, b):
        return (a.astype(jnp.float32) + b.astype(jnp.float32)).astype(jnp.bfloat16)

    def merge(c):
        for d in range(1, GROUP):
            turn_copy(c, d).wait_recv()
        for k in range(4):
            ahead_arrival(c, k).wait_recv()
        for group in (other, zhi):
            for k in range(4):
                there = jnp.minimum(k + zhi, 3)
                at = slice(k * frames, (k + 1) * frames)
                for h in range(2):
                    first = total(recv[c, 2 * k, group, h, frames:, :], recv[c, 2 * k + 1, group, h, :frames, :])
                    rest = ahead[c, there, group, h].astype(jnp.float32)
                    if k == 3:
                        rest = jnp.where(zhi == 0, rest, 0.0)
                    second = total(recv[c, 2 * k + 1, group, h, frames:, :], rest)
                    if group is other:
                        far[c, 0, h, at] = first
                        far[c, 1, h, at] = second
                    else:
                        blocks[c, i, 2 * zhi, h, at] = first
                        blocks[c, i, 2 * zhi + 1, h, at] = second
            if group is other:
                for d in (1, 3, 2):
                    far_copy(c, d).start()
        ring_start(c, 0, 0)
        for d in (2, 1, 3):
            near_copy(c, d).start()

    def spread_near(c):
        for d in (2, 1, 3):
            near_copy(c, d).wait_recv()
            ring_start(c, d, 0)

    def spread_far(c):
        for d in (1, 3, 2):
            source = lax.rem(z + NZ - d, NZ)
            far_arrival(c, source).wait_recv()
            if d == 1:
                pl.when(z >= 1)(lambda: tie_copy(c, z - 1, 0).start())
            if d == 3:
                pl.when(z == 2)(lambda: tie_copy(c, 3, 1).start())
            ring_start(c, d, 1)

    def spread_tie(c):
        far_arrival(c, z).wait_recv()
        ring_start(c, 0, 1)

    def left_rows(c, slot):
        span = 2 * blocks.shape[4]
        for seg in range(4):
            re = blocks[c, slot, seg, 0]
            im = blocks[c, slot, seg, 1]
            lt[:width, seg * span:(seg + 1) * span] = jnp.concatenate([re, im], axis=0).T
            lt[width:, seg * span:(seg + 1) * span] = jnp.concatenate([im, -re], axis=0).T

    def slot_of(column, d):
        return lax.rem(z + NZ - d, NZ) * NY + column

    def products(c, wanted, put):
        depth = 8 * blocks.shape[4]
        for n in range(0, len(wanted), 2):
            pair = wanted[n:n + 2]
            right = [blocks[c, slot_of(*where)].reshape(depth, width) for where in pair]
            prod = jnp.dot(lt[...], jnp.concatenate(right, axis=1), preferred_element_type=jnp.float32)
            prod = (prod * (2.0 / depth)).astype(jnp.bfloat16)
            for k, where in enumerate(pair):
                for h in range(2):
                    put(n + k, where, h, prod[h * width:(h + 1) * width, k * width:(k + 1) * width])

    def put_row(c):
        def put(n, where, h, value):
            at = pl.ds(pl.multiple_of(slot_of(*where) * width, width), width)
            vout[c, h, :, at] = value
        return put

    def put_send(c, side):
        def put(n, where, h, value):
            vsend[c, side, n, h] = value
        return put

    def correlate(c):
        for stage in range(2):
            y_copy(c, 0, stage).wait_recv()
        left_rows(c, z * NY + back(c))
        for stage in range(2):
            for d in BACK:
                b_copy(c, d, stage).wait_recv()
        products(c, [(y, 1), (y, 3), (fwd(c), 0), (fwd(c), 2)], put_send(c, 0))
        v_copy(c, 0).start()
        left_rows(c, z * NY + fwd(c))
        for stage in range(2):
            for d in FWD[1:]:
                y_copy(c, d, stage).wait_recv()
        products(c, [(back(c), 1), (back(c), 3), (y, 2)], put_send(c, 1))
        v_copy(c, 1).start()
        left_rows(c, i)
        here = [(y, d) for d in range(NZ)] + [(back(c), d) for d in FWD] + [(fwd(c), d) for d in BACK]
        products(c, here, put_row(c))

    def collect(c):
        across = lax.rem(y + 2, NY)
        for side in range(2):
            v_copy(c, side).wait_recv()
            got = ([(fwd(c), 1), (fwd(c), 3), (across, 0), (across, 2)], [(across, 1), (across, 3), (back(c), 2)])[side]
            for n, where in enumerate(got):
                for h in range(2):
                    put_row(c)(n, where, h, vin[c, side, n, h])
        pltpu.make_async_copy(vout.at[c], out_hbm.at[:, c], out_sem.at[c]).start()

    def channel(c):
        weights(c)
        filtered(c, 0, pairs)
        if c == 0:
            pl.semaphore_wait(barrier, len(peers) + GROUP)
        finish(c)

    channel(0)
    channel(1)
    merge(0)
    channel(2)
    spread_near(0)
    spread_far(0)
    merge(1)
    channel(3)
    spread_tie(0)
    spread_near(1)
    spread_far(1)
    merge(2)
    spread_tie(1)
    correlate(0)
    spread_near(2)
    spread_far(2)
    merge(3)
    spread_tie(2)
    correlate(1)
    spread_near(3)
    spread_far(3)
    spread_tie(3)
    collect(0)
    correlate(2)
    collect(1)
    correlate(3)
    collect(2)
    collect(3)
    for c in range(CH_DEV):
        for d in range(1, GROUP):
            turn_copy(c, d).wait_send()

        @pl.when(core == 0)
        def _():
            for member in range(GROUP):
                ahead_copy(c, member).wait_send()

        for d in range(1, NZ):
            near_copy(c, d).wait_send()
            far_copy(c, d).wait_send()
        pl.when(z >= 1)(lambda: tie_copy(c, z - 1, 0).wait_send())
        pl.when(z == 2)(lambda: tie_copy(c, 3, 1).wait_send())
        for stage in range(2):
            for d in FWD:
                y_copy(c, d, stage).wait_send()
            for d in BACK:
                b_copy(c, d, stage).wait_send()
        for side in range(2):
            v_copy(c, side).wait_send()
        pltpu.make_async_copy(vout.at[c], out_hbm.at[:, c], out_sem.at[c]).wait()


def on_device(samples, filter_taps):
    ntaps, nch = filter_taps.shape
    width = samples.shape[2]
    frames = samples.shape[1] // nch
    total = frames * TM
    rows = 2 * TM
    local = samples.reshape(2, frames, nch, width)
    dma = pltpu.SemaphoreType.DMA
    return pl.pallas_call(
        kernel,
        out_shape=jax.ShapeDtypeStruct((2, CH_DEV, width, INP * width), jnp.bfloat16),
        in_specs=[
            pl.BlockSpec(memory_space=pltpu.HBM),
            pl.BlockSpec(memory_space=pltpu.VMEM),
            pl.BlockSpec(memory_space=pltpu.VMEM),
        ],
        out_specs=pl.BlockSpec(memory_space=pl.ANY),
        scratch_shapes=[
            pltpu.VMEM((2, frames, nch, width), jnp.bfloat16),
            pltpu.VMEM((ntaps * rows, 2 * nch), jnp.bfloat16),
            pltpu.VMEM((2 * frames * rows, width), jnp.float32),
            pltpu.VMEM((CH_DEV, GROUP, 2, 2, 2 * frames, width), jnp.bfloat16),
            pltpu.VMEM((CH_DEV, GROUP, 2, 2, 2 * frames, width), jnp.bfloat16),
            pltpu.VMEM((CH_DEV, 4, 2, 2, frames, width), jnp.bfloat16),
            pltpu.VMEM((CH_DEV, 2, 2, total // 4, width), jnp.bfloat16),
            pltpu.VMEM((CH_DEV, INP, 4, 2, total // 4, width), jnp.bfloat16),
            pltpu.VMEM((2 * width, 2 * total), jnp.bfloat16),
            pltpu.VMEM((CH_DEV, 2, width, INP * width), jnp.bfloat16),
            pltpu.VMEM((CH_DEV, 2, NZ, 2, width, width), jnp.bfloat16),
            pltpu.VMEM((CH_DEV, 2, NZ, 2, width, width), jnp.bfloat16),
            dma((frames // 2,)),
            dma((CH_DEV, GROUP)),
            dma((CH_DEV, GROUP)),
            dma((CH_DEV, GROUP)),
            dma((CH_DEV, 4)),
            dma((CH_DEV, NZ)),
            dma((CH_DEV, NZ)),
            dma((CH_DEV, NZ)),
            dma((CH_DEV, NZ)),
            dma((CH_DEV, 2)),
            dma((CH_DEV, NZ, 2)),
            dma((CH_DEV, NZ, 2)),
            dma((CH_DEV, NZ, 2)),
            dma((CH_DEV, NZ, 2)),
            dma((CH_DEV, 2)),
            dma((CH_DEV, 2)),
            dma((CH_DEV,)),
        ],
        compiler_params=pltpu.CompilerParams(
            collective_id=0, has_side_effects=True, vmem_limit_bytes=48 * 1024 * 1024),
        name="correlator",
    )(local, filter_taps, jnp.asarray(trig_table(nch)))


def solution(mesh):
    in_specs = (P(None, "tm", "input"), P())
    out_specs = P(None, "tm", "input", None)
    return jax.shard_map(
        on_device, mesh=mesh, in_specs=in_specs, out_specs=out_specs, check_vma=False
    )
```
